32 devices in a mesh: rows: 8 (over y, x, core), cols: 4 (over z).
Axes of the slice: x: 2, y: 2, z: 4, core: 2. Of those that a mesh axis runs over, the one named last changes fastest.
Arguments:
- anchors: bfloat16 [8192, 8192], P('rows', 'cols'), may hold values from -64 to 64
- targets: bfloat16 [8192, 512], P('rows', 'cols'), may hold values from -6 to 6
- holdout: bfloat16 [2048, 8192], P('rows', 'cols'), may hold values from -64 to 64
Outputs:
- predicted: float32 [2048, 512], P('rows', 'cols')
The draws below stay inside these ranges and needn't reach their ends.
All inputs are finite; a program needn't handle non-finite values.
Results may differ from the reference program's by a relative error of at most 0.01.
Values may be sent and summed in bfloat16 or wider, within the bound.
A program may use at most 128 MiB of HBM per device.

```python
import math
import jax
import jax.numpy as jnp
from jax import lax

D = 8192
K = 512
ANCHORS = 8192
HOLDOUT = 2048


value_bound = 64.0


def feature_scale(key):
    top_log = math.log(1.5)
    return jnp.exp(jax.random.uniform(jax.random.fold_in(key, 101), (D,), jnp.float32, 0.0, top_log))


def scaled_rows(key, amount, salt):
    own_key = jax.random.fold_in(key, salt)
    rising = jnp.exp(math.log(2.0) * jnp.arange(amount, dtype=jnp.float32) / amount)
    jitter = jnp.exp(jax.random.uniform(jax.random.fold_in(own_key, 1), (amount,), jnp.float32, 0.0, math.log(2.0)))
    values = jnp.clip(jax.random.normal(jax.random.fold_in(own_key, 2), (amount, D), jnp.float32), -6.0, 6.0)
    scaled = 0.5 * values * (rising * jitter)[:, None] * feature_scale(key)[None, :]
    return jnp.clip(scaled, -value_bound, value_bound).astype(jnp.bfloat16)


def draw_anchors(key, part):
    return scaled_rows(key, ANCHORS, 202)


def draw_holdout(key, part):
    return scaled_rows(key, HOLDOUT, 303)


def shard_levels(stream_key, extent, shards, low, top_value):
    level, own = 1.0, jax.random.fold_in(stream_key, 6)
    for position, parts in shards:
        heights = jnp.exp(jax.random.uniform(jax.random.fold_in(own, position), (parts,), jnp.float32, low / len(shards), top_value / len(shards)))
        level = level * jnp.repeat(heights, extent[position] // parts).reshape([-1 if axis == position else 1 for axis in range(len(extent))])
    return level


def noise(key, dims, width, most, split=(), held_as=jnp.bfloat16):
    factor_of = shard_levels(key, dims, split, -0.22, 0.18) if split else 1.0
    values = jax.random.normal(key, dims, jnp.float32) * width * factor_of
    return jnp.minimum(jnp.maximum(values, -most), most).astype(held_as)


def setup_inputs(seed: int = 0) -> dict:
    splits = jax.random.split(jax.random.key(seed), 4)
    anchors = draw_anchors(jax.random.fold_in(splits[3], 71), 0)
    targets = noise(splits[1], (ANCHORS, K), 1.0, 6.0, ((0, 8), (1, 4)))
    holdout = draw_holdout(jax.random.fold_in(splits[3], 71), 0)
    return {"anchors": anchors, "targets": targets, "holdout": holdout}


ridge_weight = 1.0

def gram_of(left_mat, right_mat):
    return lax.dot_general(left_mat.astype(jnp.float32), right_mat.astype(jnp.float32), (((0,), (0,)), ((), ())), precision=lax.Precision.HIGHEST, preferred_element_type=jnp.float32)

def combine_cols(block_mat, small_mat):
    return jnp.dot(block_mat.astype(jnp.float32), small_mat.astype(jnp.float32), precision=lax.Precision.HIGHEST, preferred_element_type=jnp.float32)

def symmetric(matrix):
    return 0.5 * (matrix + matrix.T)

def solve_spd(matrix, right_side):
    factor = jnp.linalg.cholesky(matrix)
    return jax.scipy.linalg.cho_solve((factor, True), right_side)

def normal_apply(anchors, direction):
    low_copy = direction.astype(jnp.bfloat16)
    images = jnp.dot(anchors.astype(jnp.float32), low_copy.astype(jnp.float32), preferred_element_type=jnp.float32).astype(jnp.bfloat16)
    normal_back = lax.dot_general(anchors.astype(jnp.float32), images.astype(jnp.float32), (((0,), (0,)), ((), ())), preferred_element_type=jnp.float32)
    return normal_back / ANCHORS + ridge_weight * direction

def reference(anchors, targets, holdout):
    start_sum = lax.dot_general(anchors.astype(jnp.float32), targets.astype(jnp.float32), (((0,), (0,)), ((), ())), preferred_element_type=jnp.float32)
    residual = start_sum / ANCHORS
    direction = residual
    res_gram = gram_of(residual, residual)
    image_dir = normal_apply(anchors, direction)
    step_alpha = solve_spd(symmetric(gram_of(direction, image_dir)), res_gram)
    fitted = combine_cols(direction, step_alpha)
    residual = residual - combine_cols(image_dir, step_alpha)
    next_gram = gram_of(residual, residual)
    step_beta = solve_spd(symmetric(res_gram), next_gram)
    direction = residual + combine_cols(direction, step_beta)
    image_dir = normal_apply(anchors, direction)
    step_alpha = solve_spd(symmetric(gram_of(direction, image_dir)), next_gram)
    fitted = fitted + combine_cols(direction, step_alpha)
    fitted_low = fitted.astype(jnp.bfloat16)
    return jnp.dot(holdout.astype(jnp.float32), fitted_low.astype(jnp.float32), preferred_element_type=jnp.float32)
```

```python
import functools

import jax
import jax.numpy as jnp
from jax import lax
from jax.experimental import pallas as pl
from jax.experimental.pallas import tpu as pltpu
from jax.sharding import PartitionSpec as P

ridge_weight = 1.0
HIGH = lax.Precision.HIGHEST
BLOCK = 128


def contract_rows(left_mat, right_mat, precision=None):
    return lax.dot_general(
        left_mat,
        right_mat,
        (((0,), (0,)), ((), ())),
        precision=precision,
        preferred_element_type=jnp.float32,
    )


def dot_high(left_mat, right_mat):
    return jnp.dot(left_mat, right_mat, precision=HIGH, preferred_element_type=jnp.float32)


def sweep_block(work):
    lanes = lax.broadcasted_iota(jnp.int32, (BLOCK, BLOCK), 1)
    lane_row = lax.broadcasted_iota(jnp.int32, (1, BLOCK), 1)

    def step(k, carry):
        p0 = 2 * k
        p1 = p0 + 1
        full = work[...]
        r0 = work[pl.ds(p0, 1), :]
        r1 = work[pl.ds(p1, 1), :]
        c0 = jnp.sum(jnp.where(lanes == p0, full, 0.0), axis=1, keepdims=True)
        c1 = jnp.sum(jnp.where(lanes == p1, full, 0.0), axis=1, keepdims=True)
        a = jnp.sum(jnp.where(lane_row == p0, r0, 0.0), axis=1, keepdims=True)
        b = jnp.sum(jnp.where(lane_row == p1, r0, 0.0), axis=1, keepdims=True)
        c = jnp.sum(jnp.where(lane_row == p1, r1, 0.0), axis=1, keepdims=True)
        inv_a = 1.0 / a
        low = b * inv_a
        inv_s = 1.0 / (c - b * low)
        d11 = inv_s
        d01 = -low * inv_s
        d00 = inv_a - low * d01
        e0 = c0 * d00 + c1 * d01
        e1 = c0 * d01 + c1 * d11
        new = full - e0 * r0 - e1 * r1
        new = jnp.where(lanes == p0, e0, jnp.where(lanes == p1, e1, new))
        n0 = d00 * r0 + d01 * r1
        n1 = d01 * r0 + d11 * r1
        n0 = jnp.where(lane_row == p0, -d00, jnp.where(lane_row == p1, -d01, n0))
        n1 = jnp.where(lane_row == p0, -d01, jnp.where(lane_row == p1, -d11, n1))
        work[...] = new
        work[pl.ds(p0, 1), :] = n0
        work[pl.ds(p1, 1), :] = n1
        return carry

    lax.fori_loop(0, BLOCK // 2, step, 0)


def inverse_kernel(mat_ref, out_ref, work, full_row):
    size = mat_ref.shape[0]
    out_ref[...] = mat_ref[...]
    for kb in range(size // BLOCK):
        here = slice(kb * BLOCK, (kb + 1) * BLOCK)
        work[...] = out_ref[here, here]
        sweep_block(work)
        pivot = -work[...]
        row = dot_high(pivot, out_ref[here, :])
        col = out_ref[:, here]
        out_ref[:, here] = jnp.zeros((size, BLOCK), jnp.float32)
        full_row[...] = row
        full_row[:, here] = pivot
        out_ref[...] = out_ref[...] - dot_high(col, full_row[...])
        out_ref[here, :] = full_row[...]


def inverse_spd(matrix):
    size = matrix.shape[0]
    return pl.pallas_call(
        inverse_kernel,
        out_shape=jax.ShapeDtypeStruct((size, size), jnp.float32),
        in_specs=[pl.BlockSpec(memory_space=pltpu.VMEM)],
        out_specs=pl.BlockSpec(memory_space=pltpu.VMEM),
        scratch_shapes=[
            pltpu.VMEM((BLOCK, BLOCK), jnp.float32),
            pltpu.VMEM((BLOCK, size), jnp.float32),
        ],
        compiler_params=pltpu.CompilerParams(vmem_limit_bytes=16 << 20),
        cost_estimate=pl.CostEstimate(
            flops=40_000_000_000, bytes_accessed=2 * 4 * size * size, transcendentals=0
        ),
        name="inverse_spd",
    )(matrix)


def symmetric(matrix):
    return 0.5 * (matrix + matrix.T)


def exchange_kernel(axis, size, pair, reduce, gather, scale, *refs):
    refs = list(refs)
    part = refs.pop(0)
    share = refs.pop(0) if reduce else None
    full = refs.pop(0) if gather else None
    if reduce:
        mate_buf, half, got, mate_send, mate_recv, red_send, red_recv = refs[:7]
        refs = refs[7:]
    if gather:
        own_send, own_recv, pass_send, pass_recv = refs
    me = lax.axis_index(axis)
    groups = size // 2 if pair else size
    parity = me % 2 if pair else 0
    place = me // 2 if pair else me
    mate = me + 1 - 2 * parity if pair else None
    chunk = part.shape[0] // size if reduce else part.shape[0]

    def member(step, other=False):
        spot = (place + step + groups) % groups
        return 2 * spot + (1 - parity if other else parity) if pair else spot

    def rows_of(index):
        return pl.ds(pl.multiple_of(index * chunk, chunk), chunk)

    def remote(src, dst, send, recv, peer):
        return pltpu.make_async_remote_copy(
            src_ref=src,
            dst_ref=dst,
            send_sem=send,
            recv_sem=recv,
            device_id={axis: peer},
            device_id_type=pl.DeviceIdType.MESH,
        )

    barrier = pltpu.get_barrier_semaphore()
    greeted = [member(step) for step in range(1, groups)] + ([mate] if pair else [])
    for peer in greeted:
        pl.semaphore_signal(
            barrier, inc=1, device_id={axis: peer}, device_id_type=pl.DeviceIdType.MESH
        )
    pl.semaphore_wait(barrier, len(greeted))

    sent = []
    steps = list(range(1, groups))
    if reduce:
        to_mate = {}
        if pair:
            for step in steps + [0]:
                to_mate[step] = remote(
                    part.at[rows_of(member(step, True))],
                    mate_buf.at[step],
                    mate_send.at[step],
                    mate_recv.at[step],
                    mate,
                )
                to_mate[step].start()
                sent.append(to_mate[step])
        onward = {}
        for step in steps:
            peer = member(step)
            if pair:
                to_mate[step].wait_recv()
                both = part[rows_of(peer)].astype(jnp.float32) + mate_buf[step].astype(jnp.float32)
                half[step] = both.astype(half.dtype)
                source = half.at[step]
            else:
                source = part.at[rows_of(peer)]
            onward[step] = remote(source, got.at[step], red_send.at[step], red_recv.at[step], peer)
            onward[step].start()
            sent.append(onward[step])
        total = part[rows_of(me)].astype(jnp.float32)
        if pair:
            to_mate[0].wait_recv()
            total = total + mate_buf[0].astype(jnp.float32)
        share[...] = total
        for step in steps:
            onward[step].wait_recv()
            share[...] += got[step].astype(jnp.float32)
        if scale != 1.0:
            share[...] *= scale
    if gather:
        own = full.at[rows_of(me)]
        full[rows_of(me)] = (share if reduce else part)[...].astype(full.dtype)
        source = own if reduce else part
        for step in steps:
            copy = remote(source, own, own_send.at[step], own_recv.at[step], member(step))
            copy.start()
            sent.append(copy)
        passed = []
        if pair:
            copy = remote(source, own, pass_send.at[0], pass_recv.at[0], mate)
            copy.start()
            sent.append(copy)
        for step in steps:
            came = full.at[rows_of(member(-step))]
            remote(came, came, own_send.at[step], own_recv.at[step], member(step)).wait_recv()
            if pair:
                copy = remote(came, came, pass_send.at[step], pass_recv.at[step], mate)
                copy.start()
                sent.append(copy)
        if pair:
            for step in [0] + steps:
                came = full.at[rows_of(member(-step, True))]
                remote(came, came, pass_send.at[step], pass_recv.at[step], mate).wait_recv()
    for copy in sent:
        copy.wait_send()


def exchange(part, axis, identity, pair=False, reduce=True, gather=True, scale=1.0):
    size = lax.axis_size(axis)
    pair = pair and size % 2 == 0 and size > 2
    groups = size // 2 if pair else size
    rows, cols = part.shape
    chunk = rows // size if reduce else rows
    outs, scratch = [], []
    if reduce:
        outs.append(jax.ShapeDtypeStruct((chunk, cols), jnp.float32))
        slots = groups if pair else 1
        half_rows = chunk if pair else 16
        scratch += [
            pltpu.VMEM((slots, half_rows, cols), part.dtype),
            pltpu.VMEM((slots, half_rows, cols), part.dtype),
            pltpu.VMEM((groups, chunk, cols), part.dtype),
        ]
        scratch += [pltpu.SemaphoreType.DMA((groups,))] * 4
    if gather:
        outs.append(jax.ShapeDtypeStruct((chunk * size, cols), part.dtype))
        scratch += [pltpu.SemaphoreType.DMA((groups,))] * 4
    vmem = pl.BlockSpec(memory_space=pltpu.VMEM)
    result = pl.pallas_call(
        functools.partial(exchange_kernel, axis, size, pair, reduce, gather, scale),
        out_shape=outs,
        in_specs=[vmem],
        out_specs=[vmem] * len(outs),
        scratch_shapes=scratch,
        compiler_params=pltpu.CompilerParams(
            collective_id=identity, has_side_effects=True, vmem_limit_bytes=32 << 20
        ),
        cost_estimate=pl.CostEstimate(
            flops=25_000_000_000, bytes_accessed=4 * rows * cols, transcendentals=0
        ),
        name="exchange_%d" % identity,
    )(part)
    return result if len(outs) > 1 else result[0]


def on_device(anchors, targets, holdout):
    anchors_all = anchors.shape[0] * lax.axis_size("rows")
    own_cols = targets.shape[1]
    low_type = jnp.bfloat16

    def feature_sums(images, identity):
        partial = contract_rows(anchors, images).astype(low_type)
        return exchange(partial, "rows", identity, pair=True, scale=1.0 / anchors_all)

    def image_sums(low, identity, gather):
        partial = jnp.dot(anchors, low, preferred_element_type=jnp.float32).astype(low_type)
        return exchange(partial, "cols", identity, gather=gather)

    full_targets = lax.all_gather(targets, "cols", axis=1, tiled=True)
    res_share, res_low = feature_sums(full_targets, 1)
    img_share, img_low = image_sums(res_low, 2, True)
    gram_s, gram_d = lax.psum(
        (
            contract_rows(res_share, res_share, HIGH),
            contract_rows(img_share, img_share, HIGH) / anchors_all,
        ),
        ("rows", "cols"),
    )
    back_share, back_low = feature_sums(img_low, 3)
    second_share = image_sums(back_low, 4, False)
    late = jnp.concatenate(
        [
            contract_rows(img_share, second_share, HIGH) / anchors_all,
            contract_rows(second_share, second_share, HIGH) / anchors_all
            + ridge_weight * contract_rows(back_share, back_share, HIGH),
        ],
        axis=0,
    )
    late = exchange(late, "rows", 5, pair=True, gather=False)
    late = exchange(late, "cols", 6)[1]
    late = exchange(late, "rows", 7, pair=True, reduce=False)
    width = gram_s.shape[0]
    gram_e, corner = late[:width], late[width:]

    hold_pair = lax.psum(
        jnp.dot(
            holdout,
            jnp.concatenate([res_low, back_low], axis=1),
            preferred_element_type=jnp.float32,
        ),
        "cols",
    )

    first_col = lax.axis_index("cols") * own_cols

    def own(matrix):
        return lax.dynamic_slice_in_dim(matrix, first_col, own_cols, axis=1)

    lead_inv = inverse_spd(symmetric(gram_d + ridge_weight * gram_s))
    cross = gram_e + ridge_weight * gram_d
    carried = dot_high(lead_inv, cross)
    alpha = dot_high(lead_inv, own(gram_s))
    right_side = own(gram_d) - contract_rows(cross, alpha, HIGH)
    schur = corner - contract_rows(cross, carried, HIGH)
    coef_back = dot_high(inverse_spd(symmetric(schur)), right_side)
    coef_res = alpha - dot_high(carried, coef_back)
    return dot_high(hold_pair, jnp.concatenate([coef_res, coef_back], axis=0))


def solution(mesh):
    placed = (P("rows", "cols"), P("rows", "cols"), P("rows", "cols"))
    return jax.shard_map(
        on_device, mesh=mesh, in_specs=placed, out_specs=P("rows", "cols"), check_vma=False
    )
```

```python
import functools

import jax
import jax.numpy as jnp
from jax import lax
from jax.experimental import pallas as pl
from jax.experimental.pallas import tpu as pltpu
from jax.sharding import PartitionSpec as P

ridge_weight = 1.0
HIGH = lax.Precision.HIGHEST
BLOCK = 128


def contract_rows(left_mat, right_mat, precision=None):
    return lax.dot_general(
        left_mat,
        right_mat,
        (((0,), (0,)), ((), ())),
        precision=precision,
        preferred_element_type=jnp.float32,
    )


def dot_high(left_mat, right_mat):
    return jnp.dot(left_mat, right_mat, precision=HIGH, preferred_element_type=jnp.float32)


def sweep_block(work):
    lanes = lax.broadcasted_iota(jnp.int32, (BLOCK, BLOCK), 1)
    lane_row = lax.broadcasted_iota(jnp.int32, (1, BLOCK), 1)

    def step(k, carry):
        p0 = 2 * k
        p1 = p0 + 1
        full = work[...]
        r0 = work[pl.ds(p0, 1), :]
        r1 = work[pl.ds(p1, 1), :]
        c0 = jnp.sum(jnp.where(lanes == p0, full, 0.0), axis=1, keepdims=True)
        c1 = jnp.sum(jnp.where(lanes == p1, full, 0.0), axis=1, keepdims=True)
        a = jnp.sum(jnp.where(lane_row == p0, r0, 0.0), axis=1, keepdims=True)
        b = jnp.sum(jnp.where(lane_row == p1, r0, 0.0), axis=1, keepdims=True)
        c = jnp.sum(jnp.where(lane_row == p1, r1, 0.0), axis=1, keepdims=True)
        inv_a = 1.0 / a
        low = b * inv_a
        inv_s = 1.0 / (c - b * low)
        d11 = inv_s
        d01 = -low * inv_s
        d00 = inv_a - low * d01
        e0 = c0 * d00 + c1 * d01
        e1 = c0 * d01 + c1 * d11
        new = full - e0 * r0 - e1 * r1
        new = jnp.where(lanes == p0, e0, jnp.where(lanes == p1, e1, new))
        n0 = d00 * r0 + d01 * r1
        n1 = d01 * r0 + d11 * r1
        n0 = jnp.where(lane_row == p0, -d00, jnp.where(lane_row == p1, -d01, n0))
        n1 = jnp.where(lane_row == p0, -d01, jnp.where(lane_row == p1, -d11, n1))
        work[...] = new
        work[pl.ds(p0, 1), :] = n0
        work[pl.ds(p1, 1), :] = n1
        return carry

    lax.fori_loop(0, BLOCK // 2, step, 0)


def eliminate(out_ref, work, full_row, kb):
    size = out_ref.shape[0]
    here = slice(kb * BLOCK, (kb + 1) * BLOCK)
    work[...] = out_ref[here, here]
    sweep_block(work)
    pivot = -work[...]
    full_row[...] = dot_high(pivot, out_ref[here, :])
    full_row[:, here] = pivot
    col = out_ref[:, here]
    out_ref[:, here] = jnp.zeros((size, BLOCK), jnp.float32)
    out_ref[...] = out_ref[...] - dot_high(col, full_row[...])
    out_ref[here, :] = full_row[...]


def inverse_kernel(mat_ref, out_ref, work, full_row):
    out_ref[...] = mat_ref[...]
    for kb in range(mat_ref.shape[0] // BLOCK):
        eliminate(out_ref, work, full_row, kb)


def inverse_spd(matrix):
    size = matrix.shape[0]
    return pl.pallas_call(
        inverse_kernel,
        out_shape=jax.ShapeDtypeStruct((size, size), jnp.float32),
        in_specs=[pl.BlockSpec(memory_space=pltpu.VMEM)],
        out_specs=pl.BlockSpec(memory_space=pltpu.VMEM),
        scratch_shapes=[
            pltpu.VMEM((BLOCK, BLOCK), jnp.float32),
            pltpu.VMEM((BLOCK, size), jnp.float32),
        ],
        compiler_params=pltpu.CompilerParams(vmem_limit_bytes=16 << 20),
        cost_estimate=pl.CostEstimate(
            flops=40_000_000_000, bytes_accessed=2 * 4 * size * size, transcendentals=0
        ),
        name="inverse_spd",
    )(matrix)


def symmetric(matrix):
    return 0.5 * (matrix + matrix.T)


def exchange_kernel(axis, size, pair, reduce, gather, scale, blocks, *refs):
    refs = list(refs)
    part = refs.pop(0)
    mat_in = refs.pop(0) if blocks else None
    share = refs.pop(0) if reduce else None
    full = refs.pop(0) if gather else None
    if blocks:
        mat_out = refs.pop(0)
        full_row = refs.pop()
        work = refs.pop()

    def meanwhile(which):
        if which < len(blocks):
            for kb in blocks[which]:
                eliminate(mat_out, work, full_row, kb)

    if reduce:
        mate_buf, half, got, mate_send, mate_recv, red_send, red_recv = refs[:7]
        refs = refs[7:]
    if gather:
        own_send, own_recv, pass_send, pass_recv = refs
    me = lax.axis_index(axis)
    groups = size // 2 if pair else size
    parity = me % 2 if pair else 0
    place = me // 2 if pair else me
    mate = me + 1 - 2 * parity if pair else None
    chunk = part.shape[0] // size if reduce else part.shape[0]

    def member(step, other=False):
        spot = (place + step + groups) % groups
        return 2 * spot + (1 - parity if other else parity) if pair else spot

    def rows_of(index):
        return pl.ds(pl.multiple_of(index * chunk, chunk), chunk)

    def remote(src, dst, send, recv, peer):
        return pltpu.make_async_remote_copy(
            src_ref=src,
            dst_ref=dst,
            send_sem=send,
            recv_sem=recv,
            device_id={axis: peer},
            device_id_type=pl.DeviceIdType.MESH,
        )

    barrier = pltpu.get_barrier_semaphore()
    greeted = [member(step) for step in range(1, groups)] + ([mate] if pair else [])
    for peer in greeted:
        pl.semaphore_signal(
            barrier, inc=1, device_id={axis: peer}, device_id_type=pl.DeviceIdType.MESH
        )
    pl.semaphore_wait(barrier, len(greeted))
    if blocks:
        mat_out[...] = mat_in[...]

    sent = []
    steps = list(range(1, groups))
    if reduce:
        to_mate = {}
        if pair:
            for step in steps + [0]:
                to_mate[step] = remote(
                    part.at[rows_of(member(step, True))],
                    mate_buf.at[step],
                    mate_send.at[step],
                    mate_recv.at[step],
                    mate,
                )
                to_mate[step].start()
                sent.append(to_mate[step])
        onward = {}
        for step in steps:
            peer = member(step)
            if pair:
                to_mate[step].wait_recv()
                both = part[rows_of(peer)].astype(jnp.float32) + mate_buf[step].astype(jnp.float32)
                half[step] = both.astype(half.dtype)
                source = half.at[step]
            else:
                source = part.at[rows_of(peer)]
            onward[step] = remote(source, got.at[step], red_send.at[step], red_recv.at[step], peer)
            onward[step].start()
            sent.append(onward[step])
        meanwhile(0)
        total = part[rows_of(me)].astype(jnp.float32)
        if pair:
            to_mate[0].wait_recv()
            total = total + mate_buf[0].astype(jnp.float32)
        share[...] = total
        for step in steps:
            onward[step].wait_recv()
            share[...] += got[step].astype(jnp.float32)
        if scale != 1.0:
            share[...] *= scale
    if gather:
        own = full.at[rows_of(me)]
        full[rows_of(me)] = (share if reduce else part)[...].astype(full.dtype)
        source = own if reduce else part
        for step in steps:
            copy = remote(source, own, own_send.at[step], own_recv.at[step], member(step))
            copy.start()
            sent.append(copy)
        passed = []
        if pair:
            copy = remote(source, own, pass_send.at[0], pass_recv.at[0], mate)
            copy.start()
            sent.append(copy)
        meanwhile(1)
        for step in steps:
            came = full.at[rows_of(member(-step))]
            remote(came, came, own_send.at[step], own_recv.at[step], member(step)).wait_recv()
            if pair:
                copy = remote(came, came, pass_send.at[step], pass_recv.at[step], mate)
                copy.start()
                sent.append(copy)
        meanwhile(2)
        if pair:
            for step in [0] + steps:
                came = full.at[rows_of(member(-step, True))]
                remote(came, came, pass_send.at[step], pass_recv.at[step], mate).wait_recv()
    for copy in sent:
        copy.wait_send()


def exchange(part, axis, identity, pair=False, reduce=True, gather=True, scale=1.0, mat=None, blocks=()):
    size = lax.axis_size(axis)
    pair = pair and size % 2 == 0 and size > 2
    groups = size // 2 if pair else size
    rows, cols = part.shape
    chunk = rows // size if reduce else rows
    outs, scratch = [], []
    if reduce:
        outs.append(jax.ShapeDtypeStruct((chunk, cols), jnp.float32))
        slots = groups if pair else 1
        half_rows = chunk if pair else 16
        scratch += [
            pltpu.VMEM((slots, half_rows, cols), part.dtype),
            pltpu.VMEM((slots, half_rows, cols), part.dtype),
            pltpu.VMEM((groups, chunk, cols), part.dtype),
        ]
        scratch += [pltpu.SemaphoreType.DMA((groups,))] * 4
    if gather:
        outs.append(jax.ShapeDtypeStruct((chunk * size, cols), part.dtype))
        scratch += [pltpu.SemaphoreType.DMA((groups,))] * 4
    operands = [part]
    if blocks:
        width = mat.shape[0]
        operands.append(mat)
        outs.append(jax.ShapeDtypeStruct((width, width), jnp.float32))
        scratch += [
            pltpu.VMEM((BLOCK, BLOCK), jnp.float32),
            pltpu.VMEM((BLOCK, width), jnp.float32),
        ]
    vmem = pl.BlockSpec(memory_space=pltpu.VMEM)
    result = pl.pallas_call(
        functools.partial(exchange_kernel, axis, size, pair, reduce, gather, scale, blocks),
        out_shape=outs,
        in_specs=[vmem] * len(operands),
        out_specs=[vmem] * len(outs),
        scratch_shapes=scratch,
        compiler_params=pltpu.CompilerParams(
            collective_id=identity, has_side_effects=True, vmem_limit_bytes=32 << 20
        ),
        cost_estimate=pl.CostEstimate(
            flops=25_000_000_000, bytes_accessed=4 * rows * cols, transcendentals=0
        ),
        name="exchange_%d" % identity,
    )(*operands)
    return result if len(outs) > 1 else result[0]


def on_device(anchors, targets, holdout):
    anchors_all = anchors.shape[0] * lax.axis_size("rows")
    low_type = jnp.bfloat16

    def feature_sums(images, identity):
        partial = contract_rows(anchors, images).astype(low_type)
        return exchange(partial, "rows", identity, pair=True, scale=1.0 / anchors_all)

    def image_sums(low, identity, gather):
        partial = jnp.dot(anchors, low, preferred_element_type=jnp.float32).astype(low_type)
        return exchange(partial, "cols", identity, pair=True, gather=gather)

    stacked = exchange(targets, "cols", 8, pair=True, reduce=False)
    stacked = stacked.reshape(lax.axis_size("cols"), *targets.shape)
    full_targets = jnp.concatenate(list(stacked), axis=1)
    res_share, res_low = feature_sums(full_targets, 1)
    img_share, img_low = image_sums(res_low, 2, True)
    part_s = contract_rows(res_share, res_share, HIGH)
    part_d = contract_rows(img_share, img_share, HIGH) / anchors_all
    lead = lax.psum(part_d + ridge_weight * part_s, ("rows", "cols"))
    back_share, back_low = feature_sums(img_low, 3)
    second_share = image_sums(back_low, 4, False)
    late = jnp.concatenate(
        [
            contract_rows(img_share, second_share, HIGH) / anchors_all + ridge_weight * part_d,
            contract_rows(second_share, second_share, HIGH) / anchors_all
            + ridge_weight * contract_rows(back_share, back_share, HIGH),
        ],
        axis=0,
    )
    late = exchange(late, "rows", 5, pair=True, gather=False)
    blocks = lead.shape[0] // BLOCK
    order = [tuple(range(i * blocks // 4, (i + 1) * blocks // 4)) for i in range(4)]
    sides = jnp.concatenate([part_s, part_d], axis=0)
    late, lead, sides = lax.optimization_barrier((late, lead, sides))
    sides = lax.psum_scatter(sides, "cols", scatter_dimension=1, tiled=True)
    _, late, lead = exchange(
        late, "cols", 6, pair=True, mat=symmetric(lead), blocks=(order[0], order[1])
    )
    late, lead_inv = exchange(
        late, "rows", 7, pair=True, reduce=False, mat=lead, blocks=((), order[2], order[3])
    )
    late, sides = lax.optimization_barrier((late, sides))
    sides = lax.psum(sides, "rows")
    width = lead.shape[0]
    cross, corner = late[:width], late[width:]
    own_s, own_d = sides[:width], sides[width:]

    hold_pair = lax.psum(
        jnp.dot(
            holdout,
            jnp.concatenate([res_low, back_low], axis=1),
            preferred_element_type=jnp.float32,
        ),
        "cols",
    )

    carried = dot_high(lead_inv, cross)
    alpha = dot_high(lead_inv, own_s)
    right_side = own_d - contract_rows(cross, alpha, HIGH)
    schur = corner - contract_rows(cross, carried, HIGH)
    coef_back = dot_high(inverse_spd(symmetric(schur)), right_side)
    coef_res = alpha - dot_high(carried, coef_back)
    return dot_high(hold_pair, jnp.concatenate([coef_res, coef_back], axis=0))


def solution(mesh):
    placed = (P("rows", "cols"), P("rows", "cols"), P("rows", "cols"))
    return jax.shard_map(
        on_device, mesh=mesh, in_specs=placed, out_specs=P("rows", "cols"), check_vma=False
    )
```

```python
import functools

import jax
import jax.numpy as jnp
from jax import lax
from jax.experimental import pallas as pl
from jax.experimental.pallas import tpu as pltpu
from jax.sharding import PartitionSpec as P

ridge_weight = 1.0
HIGH = lax.Precision.HIGHEST
BLOCK = 128


def contract_rows(left_mat, right_mat, precision=None):
    return lax.dot_general(
        left_mat,
        right_mat,
        (((0,), (0,)), ((), ())),
        precision=precision,
        preferred_element_type=jnp.float32,
    )


def dot_high(left_mat, right_mat):
    return jnp.dot(left_mat, right_mat, precision=HIGH, preferred_element_type=jnp.float32)


def sweep_block(work):
    lanes = lax.broadcasted_iota(jnp.int32, (BLOCK, BLOCK), 1)
    lane_row = lax.broadcasted_iota(jnp.int32, (1, BLOCK), 1)

    def step(k, carry):
        p0 = 2 * k
        p1 = p0 + 1
        full = work[...]
        r0 = work[pl.ds(p0, 1), :]
        r1 = work[pl.ds(p1, 1), :]
        c0 = jnp.sum(jnp.where(lanes == p0, full, 0.0), axis=1, keepdims=True)
        c1 = jnp.sum(jnp.where(lanes == p1, full, 0.0), axis=1, keepdims=True)
        a = jnp.sum(jnp.where(lane_row == p0, r0, 0.0), axis=1, keepdims=True)
        b = jnp.sum(jnp.where(lane_row == p1, r0, 0.0), axis=1, keepdims=True)
        c = jnp.sum(jnp.where(lane_row == p1, r1, 0.0), axis=1, keepdims=True)
        inv_a = 1.0 / a
        low = b * inv_a
        inv_s = 1.0 / (c - b * low)
        d11 = inv_s
        d01 = -low * inv_s
        d00 = inv_a - low * d01
        e0 = c0 * d00 + c1 * d01
        e1 = c0 * d01 + c1 * d11
        new = full - e0 * r0 - e1 * r1
        new = jnp.where(lanes == p0, e0, jnp.where(lanes == p1, e1, new))
        n0 = d00 * r0 + d01 * r1
        n1 = d01 * r0 + d11 * r1
        n0 = jnp.where(lane_row == p0, -d00, jnp.where(lane_row == p1, -d01, n0))
        n1 = jnp.where(lane_row == p0, -d01, jnp.where(lane_row == p1, -d11, n1))
        work[...] = new
        work[pl.ds(p0, 1), :] = n0
        work[pl.ds(p1, 1), :] = n1
        return carry

    lax.fori_loop(0, BLOCK // 2, step, 0)


def inverse_kernel(mat_ref, out_ref, work, full_row):
    size = mat_ref.shape[0]
    out_ref[...] = mat_ref[...]
    for kb in range(size // BLOCK):
        here = slice(kb * BLOCK, (kb + 1) * BLOCK)
        work[...] = out_ref[here, here]
        sweep_block(work)
        pivot = -work[...]
        row = dot_high(pivot, out_ref[here, :])
        col = out_ref[:, here]
        out_ref[:, here] = jnp.zeros((size, BLOCK), jnp.float32)
        full_row[...] = row
        full_row[:, here] = pivot
        out_ref[...] = out_ref[...] - dot_high(col, full_row[...])
        out_ref[here, :] = full_row[...]


def inverse_spd(matrix):
    size = matrix.shape[0]
    return pl.pallas_call(
        inverse_kernel,
        out_shape=jax.ShapeDtypeStruct((size, size), jnp.float32),
        in_specs=[pl.BlockSpec(memory_space=pltpu.VMEM)],
        out_specs=pl.BlockSpec(memory_space=pltpu.VMEM),
        scratch_shapes=[
            pltpu.VMEM((BLOCK, BLOCK), jnp.float32),
            pltpu.VMEM((BLOCK, size), jnp.float32),
        ],
        compiler_params=pltpu.CompilerParams(vmem_limit_bytes=16 << 20),
        cost_estimate=pl.CostEstimate(
            flops=40_000_000_000, bytes_accessed=2 * 4 * size * size, transcendentals=0
        ),
        name="inverse_spd",
    )(matrix)


def symmetric(matrix):
    return 0.5 * (matrix + matrix.T)


def exchange_kernel(axis, size, pair, reduce, gather, scale, *refs):
    refs = list(refs)
    part = refs.pop(0)
    share = refs.pop(0) if reduce else None
    full = refs.pop(0) if gather else None
    if reduce:
        mate_buf, half, got, mate_send, mate_recv, red_send, red_recv = refs[:7]
        refs = refs[7:]
    if gather:
        own_send, own_recv, pass_send, pass_recv = refs
    me = lax.axis_index(axis)
    groups = size // 2 if pair else size
    parity = me % 2 if pair else 0
    place = me // 2 if pair else me
    mate = me + 1 - 2 * parity if pair else None
    chunk = part.shape[0] // size if reduce else part.shape[0]

    def member(step, other=False):
        spot = (place + step + groups) % groups
        return 2 * spot + (1 - parity if other else parity) if pair else spot

    def rows_of(index):
        return pl.ds(pl.multiple_of(index * chunk, chunk), chunk)

    def remote(src, dst, send, recv, peer):
        return pltpu.make_async_remote_copy(
            src_ref=src,
            dst_ref=dst,
            send_sem=send,
            recv_sem=recv,
            device_id={axis: peer},
            device_id_type=pl.DeviceIdType.MESH,
        )

    barrier = pltpu.get_barrier_semaphore()
    greeted = [member(step) for step in range(1, groups)] + ([mate] if pair else [])
    for peer in greeted:
        pl.semaphore_signal(
            barrier, inc=1, device_id={axis: peer}, device_id_type=pl.DeviceIdType.MESH
        )
    pl.semaphore_wait(barrier, len(greeted))

    sent = []
    steps = list(range(1, groups))
    if reduce:
        to_mate = {}
        if pair:
            for step in steps + [0]:
                to_mate[step] = remote(
                    part.at[rows_of(member(step, True))],
                    mate_buf.at[step],
                    mate_send.at[step],
                    mate_recv.at[step],
                    mate,
                )
                to_mate[step].start()
                sent.append(to_mate[step])
        onward = {}
        for step in steps:
            peer = member(step)
            if pair:
                to_mate[step].wait_recv()
                both = part[rows_of(peer)].astype(jnp.float32) + mate_buf[step].astype(jnp.float32)
                half[step] = both.astype(half.dtype)
                source = half.at[step]
            else:
                source = part.at[rows_of(peer)]
            onward[step] = remote(source, got.at[step], red_send.at[step], red_recv.at[step], peer)
            onward[step].start()
            sent.append(onward[step])
        total = part[rows_of(me)].astype(jnp.float32)
        if pair:
            to_mate[0].wait_recv()
            total = total + mate_buf[0].astype(jnp.float32)
        share[...] = total
        for step in steps:
            onward[step].wait_recv()
            share[...] += got[step].astype(jnp.float32)
        if scale != 1.0:
            share[...] *= scale
    if gather:
        own = full.at[rows_of(me)]
        full[rows_of(me)] = (share if reduce else part)[...].astype(full.dtype)
        source = own if reduce else part
        for step in steps:
            copy = remote(source, own, own_send.at[step], own_recv.at[step], member(step))
            copy.start()
            sent.append(copy)
        passed = []
        if pair:
            copy = remote(source, own, pass_send.at[0], pass_recv.at[0], mate)
            copy.start()
            sent.append(copy)
        for step in steps:
            came = full.at[rows_of(member(-step))]
            remote(came, came, own_send.at[step], own_recv.at[step], member(step)).wait_recv()
            if pair:
                copy = remote(came, came, pass_send.at[step], pass_recv.at[step], mate)
                copy.start()
                sent.append(copy)
        if pair:
            for step in [0] + steps:
                came = full.at[rows_of(member(-step, True))]
                remote(came, came, pass_send.at[step], pass_recv.at[step], mate).wait_recv()
    for copy in sent:
        copy.wait_send()


def exchange(part, axis, identity, pair=False, reduce=True, gather=True, scale=1.0):
    size = lax.axis_size(axis)
    pair = pair and size % 2 == 0 and size > 2
    groups = size // 2 if pair else size
    rows, cols = part.shape
    chunk = rows // size if reduce else rows
    outs, scratch = [], []
    if reduce:
        outs.append(jax.ShapeDtypeStruct((chunk, cols), jnp.float32))
        slots = groups if pair else 1
        half_rows = chunk if pair else 16
        scratch += [
            pltpu.VMEM((slots, half_rows, cols), part.dtype),
            pltpu.VMEM((slots, half_rows, cols), part.dtype),
            pltpu.VMEM((groups, chunk, cols), part.dtype),
        ]
        scratch += [pltpu.SemaphoreType.DMA((groups,))] * 4
    if gather:
        outs.append(jax.ShapeDtypeStruct((chunk * size, cols), part.dtype))
        scratch += [pltpu.SemaphoreType.DMA((groups,))] * 4
    vmem = pl.BlockSpec(memory_space=pltpu.VMEM)
    result = pl.pallas_call(
        functools.partial(exchange_kernel, axis, size, pair, reduce, gather, scale),
        out_shape=outs,
        in_specs=[vmem],
        out_specs=[vmem] * len(outs),
        scratch_shapes=scratch,
        compiler_params=pltpu.CompilerParams(
            collective_id=identity, has_side_effects=True, vmem_limit_bytes=32 << 20
        ),
        cost_estimate=pl.CostEstimate(
            flops=25_000_000_000, bytes_accessed=4 * rows * cols, transcendentals=0
        ),
        name="exchange_%d" % identity,
    )(part)
    return result if len(outs) > 1 else result[0]


def on_device(anchors, targets, holdout):
    anchors_all = anchors.shape[0] * lax.axis_size("rows")
    own_cols = targets.shape[1]
    low_type = jnp.bfloat16

    def feature_sums(images, identity):
        partial = contract_rows(anchors, images).astype(low_type)
        return exchange(partial, "rows", identity, pair=True, scale=1.0 / anchors_all)

    def image_sums(low, identity, gather):
        partial = jnp.dot(anchors, low, preferred_element_type=jnp.float32).astype(low_type)
        return exchange(partial, "cols", identity, pair=True, gather=gather)

    stacked = exchange(targets, "cols", 8, pair=True, reduce=False)
    stacked = stacked.reshape(lax.axis_size("cols"), *targets.shape)
    full_targets = jnp.concatenate(list(stacked), axis=1)
    res_share, res_low = feature_sums(full_targets, 1)
    img_share, img_low = image_sums(res_low, 2, True)
    gram_s, gram_d = lax.psum(
        (
            contract_rows(res_share, res_share, HIGH),
            contract_rows(img_share, img_share, HIGH) / anchors_all,
        ),
        ("rows", "cols"),
    )
    back_share, back_low = feature_sums(img_low, 3)
    second_share = image_sums(back_low, 4, False)
    late = jnp.concatenate(
        [
            contract_rows(img_share, second_share, HIGH) / anchors_all,
            contract_rows(second_share, second_share, HIGH) / anchors_all
            + ridge_weight * contract_rows(back_share, back_share, HIGH),
        ],
        axis=0,
    )
    late = exchange(late, "rows", 5, pair=True, gather=False)
    late = exchange(late, "cols", 6, pair=True)[1]
    late = exchange(late, "rows", 7, pair=True, reduce=False)
    width = gram_s.shape[0]
    gram_e, corner = late[:width], late[width:]

    hold_pair = lax.psum(
        jnp.dot(
            holdout,
            jnp.concatenate([res_low, back_low], axis=1),
            preferred_element_type=jnp.float32,
        ),
        "cols",
    )

    first_col = lax.axis_index("cols") * own_cols

    def own(matrix):
        return lax.dynamic_slice_in_dim(matrix, first_col, own_cols, axis=1)

    lead_inv = inverse_spd(symmetric(gram_d + ridge_weight * gram_s))
    cross = gram_e + ridge_weight * gram_d
    carried = dot_high(lead_inv, cross)
    alpha = dot_high(lead_inv, own(gram_s))
    right_side = own(gram_d) - contract_rows(cross, alpha, HIGH)
    schur = corner - contract_rows(cross, carried, HIGH)
    coef_back = dot_high(inverse_spd(symmetric(schur)), right_side)
    coef_res = alpha - dot_high(carried, coef_back)
    return dot_high(hold_pair, jnp.concatenate([coef_res, coef_back], axis=0))


def solution(mesh):
    placed = (P("rows", "cols"), P("rows", "cols"), P("rows", "cols"))
    return jax.shard_map(
        on_device, mesh=mesh, in_specs=placed, out_specs=P("rows", "cols"), check_vma=False
    )
```
